32 devices in a mesh: row: 8 (over z, core), col: 4 (over y, x).
Axes of the slice: x: 2, y: 2, z: 4, core: 2. Of those that a mesh axis runs over, the one named last changes fastest.
Arguments:
- sire_index: int32 [1024], P('row'), may hold values from 0 to 4095
- dam_index: int32 [1024], P('row'), may hold values from -1 to 4095, as said below
- relatives: float32 [4096, 4, 2048], P('row', None, 'col'), may hold values from 0 to 1
- factor_blocks: float32 [6, 2048, 2048], P(None, 'row', 'col'), may hold values from -0.125 to 0.125
- inverses: float32 [4, 2048, 2048], P(None, 'col'), as said below
Outputs:
- relationship: float32 [4, 2048, 1024], P(None, 'col', 'row')
- border: float32 [4, 2048, 1024], P(None, 'col', 'row')
The draws below stay inside these ranges and needn't reach their ends.
Inputs may be any that keep to these rules, and one draw needn't show every extreme that they name: `dam_index`: -1 marks an unknown dam; every other value is a row of relatives. `inverses`: lower triangular, with diagonal entries of 0.6 to 1.4.
All inputs are finite; a program needn't handle non-finite values.
Results may differ from the reference program's by a relative error of at most 0.0001.
Values sent between devices are 32-bit elements; how exact they have to be, the bound alone decides.
A program may use at most 128 MiB of HBM per device.

```python
import math
import jax
import jax.numpy as jnp
import numpy as np
from jax import lax

BLOCK = 2048
BLOCKS = 4
CALVES = 1024
ANIMALS = 4096
PAIRS = 6


def draw_dam_index(key, part):
    first, second = jax.random.split(jax.random.fold_in(key, 11))
    mothers = jax.random.randint(first, (CALVES,), 0, ANIMALS, dtype=jnp.int32)
    unknown = jax.random.randint(second, (CALVES,), 0, 8, dtype=jnp.int32)
    return jnp.where(unknown == 0, -1, mothers).astype(jnp.int32)


def draw_inverses(key, part):
    first, second = jax.random.split(jax.random.fold_in(key, 23))
    diagonal = jax.random.uniform(first, (BLOCKS, BLOCK), jnp.float32, 0.6, 1.4)
    spread = jax.random.normal(second, (BLOCKS, BLOCK, BLOCK), jnp.float32) * (0.6 / math.sqrt(BLOCK))
    rows_iota = lax.broadcasted_iota(jnp.int32, (BLOCK, BLOCK), 0)
    cols_iota = lax.broadcasted_iota(jnp.int32, (BLOCK, BLOCK), 1)
    lower = jnp.where(rows_iota > cols_iota, spread, 0.0)
    return lower + jnp.where(rows_iota == cols_iota, diagonal[:, :, None], 0.0)


def touch_ends(result, stream_key, smallest, largest):
    extent = result.shape
    place = [jax.random.randint(jax.random.fold_in(stream_key, axis), (), 0, extent[axis]) for axis in range(len(extent))]
    result = result.at[tuple(place)].set(smallest)
    longest = extent.index(max(extent))
    place[longest] = (place[longest] + 1) % extent[longest]
    return result.at[tuple(place)].set(largest)


def with_spikes(result, stream_key, source, target, parts, factor):
    owner, partner = [(jnp.arange(result.shape[position]) // (result.shape[position] // parts)).reshape([-1 if axis == position else 1 for axis in range(result.ndim)]) for position in (source, target)]
    chosen = jax.random.permutation(stream_key, parts)[partner]
    strong = (owner == chosen) | (owner == (partner + parts // 2) % parts)
    return jnp.where(strong, factor * result, result)


def level_of(own_key, shape, cuts, low, top_value):
    loudness, own = 1.0, jax.random.fold_in(own_key, 6)
    for dim, shards_of in cuts:
        steps = jnp.exp(jax.random.uniform(jax.random.fold_in(own, dim), (shards_of,), jnp.float32, low / len(cuts), top_value / len(cuts)))
        loudness = loudness * jnp.repeat(steps, shape[dim] // shards_of).reshape([-1 if axis == dim else 1 for axis in range(len(shape))])
    return loudness


def rank_table(count, lean):
    weights = [(1 << 20) // math.isqrt(standing ** lean) + 1 for standing in range(1, count + 1)]
    scale = 1 + sum(weights) // (1 << 30)
    return np.cumsum(np.array([max(1, weight // scale) for weight in weights]))


def skewed_ids(own_key, shape, count, skew):
    table = rank_table(count, skew)
    ticket = jax.random.randint(jax.random.fold_in(own_key, 1), shape, 0, int(table[count - 1]))
    standing = jnp.searchsorted(jnp.asarray(table, jnp.int32), ticket, side="right")
    return jax.random.permutation(jax.random.fold_in(own_key, 2), count)[standing].astype(jnp.int32)


def noise_with(key, dims, scale, limit, cuts, heavy, held_as=jnp.bfloat16):
    entries = scale * jax.random.normal(key, dims, jnp.float32)
    if cuts:
        entries = entries * level_of(key, dims, cuts, -0.22, 0.18)
    return jnp.clip(with_spikes(entries, jax.random.fold_in(key, 3), *heavy), -limit, limit).astype(held_as)


def setup_inputs(seed: int = 0) -> dict:
    splits = jax.random.split(jax.random.key(seed), 6)
    return {
        "sire_index": touch_ends(skewed_ids(splits[0], (CALVES,), ANIMALS, 2), jax.random.fold_in(splits[0], 3), 0, ANIMALS - 1).astype(jnp.int32),
        "dam_index": draw_dam_index(jax.random.fold_in(splits[5], 71), 0),
        "relatives": jnp.clip(1.0 * jax.random.uniform(splits[2], (ANIMALS, BLOCKS, BLOCK), jnp.float32) ** level_of(splits[2], (ANIMALS, BLOCKS, BLOCK), ((0, 8), (2, 4)), -0.2, 0.2), 0.0, 1.0),
        "factor_blocks": noise_with(splits[3], (PAIRS, BLOCK, BLOCK), (2 * BLOCK) ** -0.5, 0.125, ((1, 8), (2, 4)), (2, 1, 8, 2.0), jnp.float32),
        "inverses": draw_inverses(jax.random.fold_in(splits[5], 71), 0),
    }


def reference(sire_index, dam_index, relatives, factor_blocks, inverses):
    flat_rows = relatives.reshape(ANIMALS, BLOCKS * BLOCK)

    def parent_rows(index):
        clipped = jnp.maximum(index, 0).astype(jnp.int32)
        picked = jnp.take(flat_rows, clipped, axis=0)
        return jnp.where((index >= 0)[:, None], picked, jnp.zeros_like(picked))

    halves = 0.5 * parent_rows(sire_index) + 0.5 * parent_rows(dam_index)
    relationship = halves.T.reshape(BLOCKS, BLOCK, CALVES)
    solved = []
    for target in range(BLOCKS):
        remain = relationship[target]
        for source in range(target):
            remain = remain - jnp.dot(factor_blocks[target * (target - 1) // 2 + source], solved[source], precision=lax.Precision.HIGHEST, preferred_element_type=jnp.float32)
        solved.append(jnp.dot(inverses[target], remain, precision=lax.Precision.HIGHEST, preferred_element_type=jnp.float32))
    return relationship, jnp.stack(solved)
```

```python
import functools
import jax
import jax.numpy as jnp
from jax import lax
from jax.experimental import pallas as pl
from jax.experimental.pallas import tpu as pltpu
from jax.sharding import PartitionSpec as P

MESH = pl.DeviceIdType.MESH


def split(value):
    high = value.astype(jnp.bfloat16)
    return high, (value - high.astype(jnp.float32)).astype(jnp.bfloat16)


def split_exact(value):
    high = lax.reduce_precision(value, 8, 7)
    low = lax.reduce_precision(value - high, 8, 7)
    return high.astype(jnp.bfloat16), low.astype(jnp.bfloat16)


def mxu(left, right):
    return jnp.dot(left, right, preferred_element_type=jnp.float32)


def wide_product(left_high, left_low, right):
    right_high, right_low = split(right)
    return mxu(left_high, right_high) + (mxu(left_high, right_low) + mxu(left_low, right_high))


def narrow_product(left, right):
    width = right.shape[1]
    left_high, left_low = split(left)
    right_high, right_low = split(right)
    both = mxu(left_high, jnp.concatenate([right_high, right_low], axis=1))
    return both[:, :width] + (both[:, width:] + mxu(left_low, right_high))


def gather_start(cols, r, c, own_ref, slots, send, recv):
    copies = []
    for step in range(1, cols):
        copies.append(
            pltpu.make_async_remote_copy(
                src_ref=own_ref, dst_ref=slots.at[c], send_sem=send.at[step], recv_sem=recv.at[c],
                device_id=(r, (c + step) % cols), device_id_type=MESH,
            )
        )
    for copy in copies:
        copy.start()
    slots[c] = own_ref[...]
    return copies


def gather_wait(cols, r, c, slots, send, recv):
    for step in range(1, cols):
        source = (c + step) % cols
        slot = slots.at[source]
        pltpu.make_async_remote_copy(
            src_ref=slot, dst_ref=slot, send_sem=send.at[step], recv_sem=recv.at[source],
            device_id=(r, source), device_id_type=MESH,
        ).wait_recv()


def first_kernel(target, cols, relation_ref, inverse_hbm, out_ref, related, inverse, inv_sem, rel_send, rel_recv):
    r, c = lax.axis_index("row"), lax.axis_index("col")
    load = pltpu.make_async_copy(inverse_hbm.at[target], inverse, inv_sem)
    load.start()
    barrier = pltpu.get_barrier_semaphore()
    for step in range(1, cols):
        pl.semaphore_signal(barrier, inc=1, device_id=(r, (c + step) % cols), device_id_type=MESH)
    pl.semaphore_wait(barrier, cols - 1)
    copies = gather_start(cols, r, c, relation_ref, related, rel_send, rel_recv)
    load.wait()
    gather_wait(cols, r, c, related, rel_send, rel_recv)
    out_ref[...] = narrow_product(inverse[...], related[...].reshape(-1, relation_ref.shape[1]))
    for copy in copies:
        copy.wait_send()


def first_step(cols, relation, inverses):
    dma = pltpu.SemaphoreType.DMA
    return pl.pallas_call(
        functools.partial(first_kernel, 0, cols),
        out_shape=jax.ShapeDtypeStruct(relation.shape, jnp.float32),
        in_specs=[pl.BlockSpec(memory_space=pltpu.VMEM), pl.BlockSpec(memory_space=pl.ANY)],
        out_specs=pl.BlockSpec(memory_space=pltpu.VMEM),
        scratch_shapes=[
            pltpu.VMEM((cols,) + relation.shape, jnp.float32),
            pltpu.VMEM(inverses.shape[1:], jnp.float32),
            dma, dma((cols,)), dma((cols,)),
        ],
        compiler_params=pltpu.CompilerParams(
            collective_id=0, has_side_effects=True, vmem_limit_bytes=40 * 1024 * 1024
        ),
        cost_estimate=pl.CostEstimate(flops=10**9, bytes_accessed=60 * 10**6, transcendentals=0),
        name="first_step",
    )(relation, inverses)


def step_kernel(target, rows, cols, later, has_sum, *refs):
    refs = list(refs)
    border_ref, relation_ref, inverse_hbm = refs[:3]
    refs = refs[3:]
    factor_refs, refs = refs[: 1 + later], refs[1 + later :]
    if has_sum:
        sum_refs, refs = refs[: 1 + later], refs[1 + later :]
    else:
        sum_refs = None
    out_ref, refs = refs[0], refs[1:]
    sum_outs, refs = refs[:later], refs[later:]
    (
        calves, partial, landed, reduced, whole, inverse, related,
        inv_sem, rel_send, rel_recv, chip_send, chip_recv, core_send, core_recv,
        red_send, red_recv, swap_send, swap_recv, wide_send, wide_recv,
    ) = refs
    r, c = lax.axis_index("row"), lax.axis_index("col")
    chips = rows // 2
    z, core = r // 2, r % 2
    partner = 2 * z + 1 - core
    width = border_ref.shape[1]
    short = reduced.shape[0]

    load = pltpu.make_async_copy(inverse_hbm.at[target], inverse, inv_sem)
    load.start()

    barrier = pltpu.get_barrier_semaphore()
    for step in range(1, rows):
        pl.semaphore_signal(barrier, inc=1, device_id=((r + step) % rows, c), device_id_type=MESH)
    for step in range(1, cols):
        pl.semaphore_signal(barrier, inc=1, device_id=(r, (c + step) % cols), device_id_type=MESH)
    pl.semaphore_wait(barrier, rows + cols - 2)

    def lanes(owner):
        return pl.ds(pl.multiple_of(owner * width, width), width)

    def remote(src, dst, send, recv, target):
        return pltpu.make_async_remote_copy(
            src_ref=src, dst_ref=dst, send_sem=send, recv_sem=recv, device_id=target, device_id_type=MESH
        )

    own = calves.at[:, lanes(r)]
    first = [remote(border_ref, own, chip_send.at[0], core_recv.at[z], (partner, c))]
    for step in range(1, chips):
        there = (z + step) % chips
        first.append(remote(border_ref, own, chip_send.at[step], chip_recv.at[z], (2 * there + core, c)))
    for copy in first:
        copy.start()
    fifth = gather_start(cols, r, c, relation_ref, related, rel_send, rel_recv)
    calves[:, lanes(r)] = border_ref[...]
    second = []
    for step in range(1, chips):
        source = (z + step) % chips
        slot = calves.at[:, lanes(2 * source + core)]
        remote(slot, slot, chip_send.at[step], chip_recv.at[source], (partner, c)).wait_recv()
        copy = remote(slot, slot, core_send.at[step], core_recv.at[source], (partner, c))
        copy.start()
        second.append(copy)
    for step in range(chips):
        source = (z + step) % chips
        slot = calves.at[:, lanes(2 * source + 1 - core)]
        remote(slot, slot, core_send.at[step], core_recv.at[source], (partner, c)).wait_recv()

    tile = 2 * width

    def multiply(factor_ref, sum_ref, result):
        high, low = split(factor_ref[...])

        def body(index, carry):
            span = pl.ds(pl.multiple_of(index * tile, tile), tile)
            value = wide_product(high, low, calves[:, span])
            if sum_ref is not None:
                value = value + sum_ref[:, span]
            result[:, span] = value
            return carry

        lax.fori_loop(0, calves.shape[1] // tile, body, 0)

    multiply(factor_refs[0], sum_refs[0] if has_sum else None, partial)

    def band(owner):
        return pl.ds(pl.multiple_of(owner * short, short), short)

    third = []
    for step in range(1, cols):
        there = (c + step) % cols
        copy = remote(partial.at[band(there), :], landed.at[c], red_send.at[step], red_recv.at[c], (r, there))
        copy.start()
        third.append(copy)
    for index in range(later):
        multiply(factor_refs[1 + index], sum_refs[1 + index] if has_sum else None, sum_outs[index])
    total = partial[band(c), :]
    for step in range(1, cols):
        source = (c + step) % cols
        slot = landed.at[source]
        remote(slot, slot, red_send.at[step], red_recv.at[source], (r, source)).wait_recv()
        total = total + landed[source]
    reduced[...] = total

    fourth = []
    for step in range(1, rows):
        there = (r + step) % rows
        copy = remote(reduced.at[:, lanes(there)], whole.at[r, c], swap_send.at[step], swap_recv.at[r], (there, c))
        copy.start()
        fourth.append(copy)
    whole[r, c] = reduced[:, lanes(r)]

    def spread(source, action):
        for step in range(1, cols):
            there = (c + step) % cols
            slot = whole.at[source, c]
            action(remote(slot, slot, wide_send.at[source, step], wide_recv.at[source, c], (r, there)))

    spread(r, lambda copy: copy.start())
    for step in range(1, rows):
        source = (r + step) % rows
        slot = whole.at[source, c]
        remote(slot, slot, swap_send.at[step], swap_recv.at[source], (source, c)).wait_recv()
        spread(source, lambda copy: copy.start())
    for source in range(rows):
        for step in range(1, cols):
            there = (c + step) % cols
            slot = whole.at[source, there]
            remote(slot, slot, wide_send.at[source, step], wide_recv.at[source, there], (r, there)).wait_recv()

    load.wait()
    gather_wait(cols, r, c, related, rel_send, rel_recv)
    remain = (related[...] - whole[...].reshape(related.shape)).reshape(-1, width)
    out_ref[...] = narrow_product(inverse[...], remain)

    for copy in first + second + third + fourth + fifth:
        copy.wait_send()
    for source in range(rows):
        spread(source, lambda copy: copy.wait_send())


def block_step(rows, cols, target, border, relation, inverses, factors, sums):
    later = len(factors) - 1
    band, depth = factors[0].shape
    width = border.shape[1]
    short = band // cols
    dma = pltpu.SemaphoreType.DMA
    f32 = jnp.float32
    vmem = pl.BlockSpec(memory_space=pltpu.VMEM)
    out = pl.pallas_call(
        functools.partial(step_kernel, target, rows, cols, later, bool(sums)),
        out_shape=[jax.ShapeDtypeStruct(border.shape, f32)]
        + [jax.ShapeDtypeStruct((band, rows * width), f32)] * later,
        in_specs=[vmem, vmem, pl.BlockSpec(memory_space=pl.ANY)] + [vmem] * (len(factors) + len(sums)),
        out_specs=[vmem] * (1 + later),
        scratch_shapes=[
            pltpu.VMEM((depth, rows * width), f32),
            pltpu.VMEM((band, rows * width), f32),
            pltpu.VMEM((cols, short, rows * width), f32),
            pltpu.VMEM((short, rows * width), f32),
            pltpu.VMEM((rows, cols, short, width), f32),
            pltpu.VMEM(inverses.shape[1:], f32),
            pltpu.VMEM((cols,) + relation.shape, f32),
            dma, dma((cols,)), dma((cols,)),
            dma((rows // 2,)), dma((rows // 2,)), dma((rows // 2,)), dma((rows // 2,)),
            dma((cols,)), dma((cols,)), dma((rows,)), dma((rows,)), dma((rows, cols)), dma((rows, cols)),
        ],
        compiler_params=pltpu.CompilerParams(
            collective_id=target, has_side_effects=True, vmem_limit_bytes=40 * 1024 * 1024
        ),
        cost_estimate=pl.CostEstimate(flops=10**9, bytes_accessed=200 * 10**6, transcendentals=0),
        name="block_step_%d" % target,
    )(border, relation, inverses, *factors, *sums)
    return out[0], list(out[1:])


def per_device(rows, cols, sire_index, dam_index, relatives, factor_blocks, inverses):
    calf_dev = sire_index.shape[0]
    old_dev, blocks, block_cols = relatives.shape
    both = lax.all_gather(jnp.stack([sire_index, dam_index]), "row", axis=1, tiled=True)
    owned = lax.axis_index("row") * old_dev + lax.iota(jnp.int32, old_dev)
    picks = 0.5 * (
        (both[0][:, None] == owned[None, :]).astype(jnp.float32)
        + (both[1][:, None] == owned[None, :]).astype(jnp.float32)
    )
    picks = picks.astype(jnp.bfloat16)
    relationship = []
    for target in range(blocks):
        high, low = split_exact(relatives[:, target, :])
        shares = mxu(picks, high) + mxu(picks, low)
        relationship.append(lax.psum_scatter(shares, "row", scatter_dimension=0, tiled=True).T)
    solved = [first_step(cols, relationship[0], inverses)]
    sums = []
    for target in range(1, blocks):
        source = target - 1
        factors = [factor_blocks[t * (t - 1) // 2 + source] for t in range(target, blocks)]
        border, sums = block_step(
            rows, cols, target, solved[-1], relationship[target], inverses, factors, sums
        )
        solved.append(border)
    relationship, last = lax.optimization_barrier((relationship, solved[-1]))
    return (jnp.stack(relationship), jnp.stack(solved[:-1] + [last]))


def solution(mesh):
    return jax.shard_map(
        functools.partial(per_device, mesh.shape["row"], mesh.shape["col"]),
        mesh=mesh,
        in_specs=(
            P("row"),
            P("row"),
            P("row", None, "col"),
            P(None, "row", "col"),
            P(None, "col", None),
        ),
        out_specs=(P(None, "col", "row"), P(None, "col", "row")),
        check_vma=False,
    )
```

```python
import functools
import jax
import jax.numpy as jnp
from jax import lax
from jax.experimental import pallas as pl
from jax.experimental.pallas import tpu as pltpu
from jax.sharding import PartitionSpec as P

MESH = pl.DeviceIdType.MESH


def split(value):
    high = value.astype(jnp.bfloat16)
    return high, (value - high.astype(jnp.float32)).astype(jnp.bfloat16)


def split_exact(value):
    high = lax.reduce_precision(value, 8, 7)
    low = lax.reduce_precision(value - high, 8, 7)
    return high.astype(jnp.bfloat16), low.astype(jnp.bfloat16)


def mxu(left, right):
    return jnp.dot(left, right, preferred_element_type=jnp.float32)


def wide_product(left_high, left_low, right):
    right_high, right_low = split(right)
    return mxu(left_high, right_high) + (mxu(left_high, right_low) + mxu(left_low, right_high))


def narrow_product(left, right):
    width = right.shape[1]
    left_high, left_low = split(left)
    right_high, right_low = split(right)
    both = mxu(left_high, jnp.concatenate([right_high, right_low], axis=1))
    return both[:, :width] + (both[:, width:] + mxu(left_low, right_high))


def gather_start(cols, r, c, own_ref, slots, send, recv):
    copies = []
    for step in range(1, cols):
        copies.append(
            pltpu.make_async_remote_copy(
                src_ref=own_ref, dst_ref=slots.at[c], send_sem=send.at[step], recv_sem=recv.at[c],
                device_id=(r, (c + step) % cols), device_id_type=MESH,
            )
        )
    for copy in copies:
        copy.start()
    slots[c] = own_ref[...]
    return copies


def gather_wait(cols, r, c, slots, send, recv):
    for step in range(1, cols):
        source = (c + step) % cols
        slot = slots.at[source]
        pltpu.make_async_remote_copy(
            src_ref=slot, dst_ref=slot, send_sem=send.at[step], recv_sem=recv.at[source],
            device_id=(r, source), device_id_type=MESH,
        ).wait_recv()


def first_kernel(target, cols, relation_ref, inverse_hbm, out_ref, related, inverse, inv_sem, rel_send, rel_recv):
    r, c = lax.axis_index("row"), lax.axis_index("col")
    load = pltpu.make_async_copy(inverse_hbm.at[target], inverse, inv_sem)
    load.start()
    barrier = pltpu.get_barrier_semaphore()
    for step in range(1, cols):
        pl.semaphore_signal(barrier, inc=1, device_id=(r, (c + step) % cols), device_id_type=MESH)
    pl.semaphore_wait(barrier, cols - 1)
    copies = gather_start(cols, r, c, relation_ref, related, rel_send, rel_recv)
    load.wait()
    gather_wait(cols, r, c, related, rel_send, rel_recv)
    out_ref[...] = narrow_product(inverse[...], related[...].reshape(-1, relation_ref.shape[1]))
    for copy in copies:
        copy.wait_send()


def first_step(cols, relation, inverses):
    dma = pltpu.SemaphoreType.DMA
    return pl.pallas_call(
        functools.partial(first_kernel, 0, cols),
        out_shape=jax.ShapeDtypeStruct(relation.shape, jnp.float32),
        in_specs=[pl.BlockSpec(memory_space=pltpu.VMEM), pl.BlockSpec(memory_space=pl.ANY)],
        out_specs=pl.BlockSpec(memory_space=pltpu.VMEM),
        scratch_shapes=[
            pltpu.VMEM((cols,) + relation.shape, jnp.float32),
            pltpu.VMEM(inverses.shape[1:], jnp.float32),
            dma, dma((cols,)), dma((cols,)),
        ],
        compiler_params=pltpu.CompilerParams(
            collective_id=0, has_side_effects=True, vmem_limit_bytes=40 * 1024 * 1024
        ),
        cost_estimate=pl.CostEstimate(flops=10**9, bytes_accessed=60 * 10**6, transcendentals=0),
        name="first_step",
    )(relation, inverses)


def step_kernel(target, rows, cols, later, has_sum, *refs):
    refs = list(refs)
    border_ref, relation_ref, inverse_hbm = refs[:3]
    refs = refs[3:]
    factor_refs, refs = refs[: 1 + later], refs[1 + later :]
    if has_sum:
        sum_refs, refs = refs[: 1 + later], refs[1 + later :]
    else:
        sum_refs = None
    out_ref, refs = refs[0], refs[1:]
    sum_outs, refs = refs[:later], refs[later:]
    (
        calves, partial, landed, reduced, whole, inverse, related,
        inv_sem, rel_send, rel_recv, chip_send, chip_recv, core_send, core_recv,
        red_send, red_recv, swap_send, swap_recv, wide_send, wide_recv,
    ) = refs
    r, c = lax.axis_index("row"), lax.axis_index("col")
    chips = rows // 2
    z, core = r // 2, r % 2
    partner = 2 * z + 1 - core
    width = border_ref.shape[1]
    short = reduced.shape[0]

    load = pltpu.make_async_copy(inverse_hbm.at[target], inverse, inv_sem)
    load.start()

    barrier = pltpu.get_barrier_semaphore()
    for step in range(1, rows):
        pl.semaphore_signal(barrier, inc=1, device_id=((r + step) % rows, c), device_id_type=MESH)
    for step in range(1, cols):
        pl.semaphore_signal(barrier, inc=1, device_id=(r, (c + step) % cols), device_id_type=MESH)
    pl.semaphore_wait(barrier, rows + cols - 2)

    def lanes(owner):
        return pl.ds(pl.multiple_of(owner * width, width), width)

    def remote(src, dst, send, recv, target):
        return pltpu.make_async_remote_copy(
            src_ref=src, dst_ref=dst, send_sem=send, recv_sem=recv, device_id=target, device_id_type=MESH
        )

    own = calves.at[:, lanes(r)]
    first = [remote(border_ref, own, chip_send.at[0], core_recv.at[z], (partner, c))]
    for step in range(1, chips):
        there = (z + step) % chips
        first.append(remote(border_ref, own, chip_send.at[step], chip_recv.at[z], (2 * there + core, c)))
    for copy in first:
        copy.start()
    fifth = gather_start(cols, r, c, relation_ref, related, rel_send, rel_recv)
    calves[:, lanes(r)] = border_ref[...]
    second = []
    for step in range(1, chips):
        source = (z + step) % chips
        slot = calves.at[:, lanes(2 * source + core)]
        remote(slot, slot, chip_send.at[step], chip_recv.at[source], (partner, c)).wait_recv()
        copy = remote(slot, slot, core_send.at[step], core_recv.at[source], (partner, c))
        copy.start()
        second.append(copy)
    for step in range(chips):
        source = (z + step) % chips
        slot = calves.at[:, lanes(2 * source + 1 - core)]
        remote(slot, slot, core_send.at[step], core_recv.at[source], (partner, c)).wait_recv()

    tile = 2 * width

    def multiply(factor_ref, sum_ref, result):
        high, low = split(factor_ref[...])

        def body(index, carry):
            span = pl.ds(pl.multiple_of(index * tile, tile), tile)
            value = wide_product(high, low, calves[:, span])
            if sum_ref is not None:
                value = value + sum_ref[:, span]
            result[:, span] = value
            return carry

        lax.fori_loop(0, calves.shape[1] // tile, body, 0)

    multiply(factor_refs[0], sum_refs[0] if has_sum else None, partial)

    def band(owner):
        return pl.ds(pl.multiple_of(owner * short, short), short)

    third = []
    for step in range(1, cols):
        there = (c + step) % cols
        copy = remote(partial.at[band(there), :], landed.at[c], red_send.at[step], red_recv.at[c], (r, there))
        copy.start()
        third.append(copy)
    for index in range(later):
        multiply(factor_refs[1 + index], sum_refs[1 + index] if has_sum else None, sum_outs[index])
    total = partial[band(c), :]
    for step in range(1, cols):
        source = (c + step) % cols
        slot = landed.at[source]
        remote(slot, slot, red_send.at[step], red_recv.at[source], (r, source)).wait_recv()
        total = total + landed[source]
    reduced[...] = total

    fourth = []
    for step in range(1, rows):
        there = (r + step) % rows
        copy = remote(reduced.at[:, lanes(there)], whole.at[r, c], swap_send.at[step], swap_recv.at[r], (there, c))
        copy.start()
        fourth.append(copy)
    whole[r, c] = reduced[:, lanes(r)]

    def spread(source, action):
        for step in range(1, cols):
            there = (c + step) % cols
            slot = whole.at[source, c]
            action(remote(slot, slot, wide_send.at[source, step], wide_recv.at[source, c], (r, there)))

    spread(r, lambda copy: copy.start())
    for step in range(1, rows):
        source = (r + step) % rows
        slot = whole.at[source, c]
        remote(slot, slot, swap_send.at[step], swap_recv.at[source], (source, c)).wait_recv()
        spread(source, lambda copy: copy.start())
    for source in range(rows):
        for step in range(1, cols):
            there = (c + step) % cols
            slot = whole.at[source, there]
            remote(slot, slot, wide_send.at[source, step], wide_recv.at[source, there], (r, there)).wait_recv()

    load.wait()
    gather_wait(cols, r, c, related, rel_send, rel_recv)
    remain = (related[...] - whole[...].reshape(related.shape)).reshape(-1, width)
    out_ref[...] = narrow_product(inverse[...], remain)

    for copy in first + second + third + fourth + fifth:
        copy.wait_send()
    for source in range(rows):
        spread(source, lambda copy: copy.wait_send())


def block_step(rows, cols, target, border, relation, inverses, factors, sums):
    later = len(factors) - 1
    band, depth = factors[0].shape
    width = border.shape[1]
    short = band // cols
    dma = pltpu.SemaphoreType.DMA
    f32 = jnp.float32
    vmem = pl.BlockSpec(memory_space=pltpu.VMEM)
    out = pl.pallas_call(
        functools.partial(step_kernel, target, rows, cols, later, bool(sums)),
        out_shape=[jax.ShapeDtypeStruct(border.shape, f32)]
        + [jax.ShapeDtypeStruct((band, rows * width), f32)] * later,
        in_specs=[vmem, vmem, pl.BlockSpec(memory_space=pl.ANY)] + [vmem] * (len(factors) + len(sums)),
        out_specs=[vmem] * (1 + later),
        scratch_shapes=[
            pltpu.VMEM((depth, rows * width), f32),
            pltpu.VMEM((band, rows * width), f32),
            pltpu.VMEM((cols, short, rows * width), f32),
            pltpu.VMEM((short, rows * width), f32),
            pltpu.VMEM((rows, cols, short, width), f32),
            pltpu.VMEM(inverses.shape[1:], f32),
            pltpu.VMEM((cols,) + relation.shape, f32),
            dma, dma((cols,)), dma((cols,)),
            dma((rows // 2,)), dma((rows // 2,)), dma((rows // 2,)), dma((rows // 2,)),
            dma((cols,)), dma((cols,)), dma((rows,)), dma((rows,)), dma((rows, cols)), dma((rows, cols)),
        ],
        compiler_params=pltpu.CompilerParams(
            collective_id=target, has_side_effects=True, vmem_limit_bytes=40 * 1024 * 1024
        ),
        cost_estimate=pl.CostEstimate(flops=10**9, bytes_accessed=200 * 10**6, transcendentals=0),
        name="block_step_%d" % target,
    )(border, relation, inverses, *factors, *sums)
    return out[0], list(out[1:])


def per_device(rows, cols, sire_index, dam_index, relatives, factor_blocks, inverses):
    calf_dev = sire_index.shape[0]
    old_dev, blocks, block_cols = relatives.shape
    both = lax.all_gather(jnp.stack([sire_index, dam_index]), "row", axis=1, tiled=True)
    owned = lax.axis_index("row") * old_dev + lax.iota(jnp.int32, old_dev)
    picks = 0.5 * (
        (both[0][:, None] == owned[None, :]).astype(jnp.float32)
        + (both[1][:, None] == owned[None, :]).astype(jnp.float32)
    )
    picks = picks.astype(jnp.bfloat16)
    flat_rows = relatives.reshape(old_dev, blocks * block_cols)
    relationship = []
    for target in range(blocks):
        high, low = split_exact(flat_rows[:, target * block_cols : (target + 1) * block_cols])
        shares = mxu(picks, high) + mxu(picks, low)
        relationship.append(lax.psum_scatter(shares, "row", scatter_dimension=0, tiled=True).T)
    solved = [first_step(cols, relationship[0], inverses)]
    sums = []
    for target in range(1, blocks):
        source = target - 1
        factors = [factor_blocks[t * (t - 1) // 2 + source] for t in range(target, blocks)]
        border, sums = block_step(
            rows, cols, target, solved[-1], relationship[target], inverses, factors, sums
        )
        solved.append(border)
    relationship, last = lax.optimization_barrier((relationship, solved[-1]))
    return (jnp.stack(relationship), jnp.stack(solved[:-1] + [last]))


def solution(mesh):
    return jax.shard_map(
        functools.partial(per_device, mesh.shape["row"], mesh.shape["col"]),
        mesh=mesh,
        in_specs=(
            P("row"),
            P("row"),
            P("row", None, "col"),
            P(None, "row", "col"),
            P(None, "col", None),
        ),
        out_specs=(P(None, "col", "row"), P(None, "col", "row")),
        check_vma=False,
    )
```
